32 devices in a mesh: sat: 8 (over z, x), tm: 4 (over y, core).
Axes of the slice: x: 2, y: 2, z: 4, core: 2. Of those that a mesh axis runs over, the one named last changes fastest.
Arguments:
- panels: bfloat16 [64, 32, 64, 128], P('sat', 'tm'), may hold values from -0.3125 to 0.3125
- weights: bfloat16 [64, 32, 64], P('sat', 'tm'), may hold values from 0.19921875 to 5
- pair_members: int32 [32, 2], P('sat'), may hold values from 0 to 63, as said below
- pair_live: int32 [32, 32], P('tm', 'sat'), may hold values 0 or 1
Outputs:
- normal_rows: float32 [12288, 128], P(('sat', 'tm'))
The draws below stay inside these ranges and needn't reach their ends.
Inputs may be any that keep to these rules, and one draw needn't show every extreme that they name: `pair_members`: every satellite is a member of exactly one baseline, and both members of baseline p are satellites whose numbers leave the remainder p // 4 when divided by 8.
All inputs are finite; a program needn't handle non-finite values. No bound on the sum of `pair_live` on one device may be relied on, other than what follows from the above.
Results may differ from the reference program's by a relative error of at most 0.0009.
Values may be sent and summed in bfloat16 or wider, within the bound.
A program may use at most 64 MiB of HBM per device.

```python
import math
import jax
import jax.numpy as jnp
from jax import lax

P_SIZE = 128
K = 64
SAT_DEV = 8
NSAT = 64
NPAIR = 32
NEPB = 32


def draw_pair_members(key, part):
    group_count = SAT_DEV
    scores = jax.random.randint(jax.random.fold_in(key, 29), (group_count, group_count), 0, 1 << 20)
    scores = scores * group_count + jnp.arange(group_count, dtype=jnp.int32)[None, :]
    ordering = jnp.argsort(scores, axis=1).astype(jnp.int32)
    owners = jnp.arange(group_count, dtype=jnp.int32)[:, None]
    members = ordering * group_count + owners
    return members.reshape(NPAIR, 2).astype(jnp.int32)


def touch_ends(values, own_key, low, high):
    dims = values.shape
    spot = [jax.random.randint(jax.random.fold_in(own_key, axis), (), 0, dims[axis]) for axis in range(len(dims))]
    values = values.at[tuple(spot)].set(low)
    longest = dims.index(max(dims))
    spot[longest] = (spot[longest] + 1) % dims[longest]
    return values.at[tuple(spot)].set(high)


def block_levels(rng, extent, cuts, least, largest):
    level, own = 1.0, jax.random.fold_in(rng, 6)
    for axis_at, shards_of in cuts:
        heights = jnp.exp(jax.random.uniform(jax.random.fold_in(own, axis_at), (shards_of,), jnp.float32, least / len(cuts), largest / len(cuts)))
        level = level * jnp.repeat(heights, extent[axis_at] // shards_of).reshape([-1 if axis == axis_at else 1 for axis in range(len(extent))])
    return level


def scatter_about(key, dims, width, bound, pieces=(), kind=jnp.bfloat16):
    entries = width * jax.random.normal(key, dims, jnp.float32)
    if pieces:
        entries = entries * block_levels(key, dims, pieces, -0.22, 0.18)
    return jnp.clip(entries, -bound, bound).astype(kind)


def setup_inputs(seed: int = 0) -> dict:
    key_of = jax.random.split(jax.random.key(seed), 5)
    panels = scatter_about(key_of[0], (NSAT, NEPB, K, P_SIZE), ((1.0 / (NEPB * K)) ** 0.5), 0.3125, ((0, 8), (1, 4)))
    weights = jnp.clip(jnp.exp(math.log(5.0) - 3.2227897 * jax.random.uniform(key_of[1], (NSAT, NEPB, K), jnp.float32) ** block_levels(key_of[1], (NSAT, NEPB, K), ((0, 8), (1, 4)), -0.2, 0.2)), 0.19921875, 5.0).astype(jnp.bfloat16)
    pair_members = draw_pair_members(jax.random.fold_in(key_of[4], 71), 0)
    pair_live = touch_ends((jax.random.randint(key_of[3], (NEPB, NPAIR), 0, 4) < 3).astype(jnp.int32), jax.random.fold_in(key_of[3], 1), 0, 1)
    return dict(panels=panels, weights=weights, pair_members=pair_members, pair_live=pair_live)


def scale_rows(root_weight, panel):
    scaled = (root_weight[:, :, None] * panel.astype(jnp.float32)).astype(jnp.bfloat16)
    scaled = lax.optimization_barrier(scaled)
    return scaled.astype(jnp.float32).reshape(-1, panel.shape[-1])

def gram(left_rows, right_rows):
    return lax.dot_general(left_rows, right_rows, (((0,), (0,)), ((), ())), precision=lax.Precision.HIGHEST, preferred_element_type=jnp.float32)

def pair_blocks(first_panel, second_panel, first_weight, second_weight, live_pair):
    first_value = first_weight.astype(jnp.float32)
    second_value = second_weight.astype(jnp.float32)
    dd_weight = live_pair[:, None] * first_value * second_value / (first_value + second_value)
    root_weight = jnp.sqrt(dd_weight)
    first_scaled = scale_rows(root_weight, first_panel)
    second_scaled = scale_rows(root_weight, second_panel)
    first_gram = gram(first_scaled, first_scaled)
    cross_gram = -gram(first_scaled, second_scaled)
    second_gram = gram(second_scaled, second_scaled)
    return jnp.stack([first_gram, cross_gram, second_gram], axis=0)

def reference(panels, weights, pair_members, pair_live):
    params = panels.shape[-1]

    def one_pair(pair_no):
        first_id = pair_members[pair_no, 0].astype(jnp.int32)
        second_id = pair_members[pair_no, 1].astype(jnp.int32)
        first_panel = lax.dynamic_index_in_dim(panels, first_id, 0, keepdims=False)
        second_panel = lax.dynamic_index_in_dim(panels, second_id, 0, keepdims=False)
        first_weight = lax.dynamic_index_in_dim(weights, first_id, 0, keepdims=False)
        second_weight = lax.dynamic_index_in_dim(weights, second_id, 0, keepdims=False)
        live_pair = lax.dynamic_index_in_dim(pair_live, pair_no, 1, keepdims=False).astype(jnp.float32)
        return pair_blocks(first_panel, second_panel, first_weight, second_weight, live_pair)
    blocks = lax.map(one_pair, jnp.arange(NPAIR, dtype=jnp.int32))
    return blocks.reshape(NPAIR * 3 * params, params)
```

```python
import functools
import jax
import jax.numpy as jnp
from jax import lax
from jax.experimental import pallas as pl
from jax.experimental.pallas import tpu as pltpu
from jax.sharding import PartitionSpec as P

MESH = pl.DeviceIdType.MESH
CHUNKS = 4


def kernel(nsat, ntm, panels, weights, members, live_ref, out_ref, *scratch):
    held = scratch[:CHUNKS]
    (heldw, root_ref, scaled, acc, gram, arrived,
     psend, precv, wsend, wrecv, gsend, grecv) = scratch[CHUNKS:]
    epochs, rows, params = panels.shape[1:]
    pairs = members.shape[0]
    per_owner = pairs // ntm
    step = epochs // CHUNKS
    s = lax.axis_index("sat")
    t = lax.axis_index("tm")

    barrier = pltpu.get_barrier_semaphore()

    def greet(axis, me, n):
        def body(k, carry):
            pl.semaphore_signal(barrier, inc=1, device_id={axis: lax.rem(me + k, n)}, device_id_type=MESH)
            return carry
        lax.fori_loop(1, n, body, 0)

    greet("sat", s, nsat)
    greet("tm", t, ntm)

    def weight_copy(k):
        dest = lax.rem(s + k, nsat)
        return pltpu.make_async_remote_copy(
            src_ref=weights.at[dest], dst_ref=heldw.at[s],
            send_sem=wsend.at[k], recv_sem=wrecv.at[k],
            device_id={"sat": dest}, device_id_type=MESH)

    def weight_arrival(k):
        source = lax.rem(s + nsat - k, nsat)
        return pltpu.make_async_remote_copy(
            src_ref=weights.at[s], dst_ref=heldw.at[source],
            send_sem=wsend.at[k], recv_sem=wrecv.at[k],
            device_id={"sat": source}, device_id_type=MESH)

    def panel_copy(c, k):
        dest = lax.rem(s + k, nsat)
        part = pl.ds(c * step, step)
        return pltpu.make_async_remote_copy(
            src_ref=panels.at[dest, part], dst_ref=held[c].at[s],
            send_sem=psend.at[c, k], recv_sem=precv.at[c, k],
            device_id={"sat": dest}, device_id_type=MESH)

    def panel_arrival(c, k):
        source = lax.rem(s + nsat - k, nsat)
        part = pl.ds(c * step, step)
        return pltpu.make_async_remote_copy(
            src_ref=panels.at[s, part], dst_ref=held[c].at[source],
            send_sem=psend.at[c, k], recv_sem=precv.at[c, k],
            device_id={"sat": source}, device_id_type=MESH)

    own_panels = [
        pltpu.make_async_copy(panels.at[s, pl.ds(c * step, step)], held[c].at[s], psend.at[c, 0])
        for c in range(CHUNKS)
    ]
    own_weight = pltpu.make_async_copy(weights.at[s], heldw.at[s], wsend.at[0])
    for copy in own_panels:
        copy.start()
    own_weight.start()

    pl.semaphore_wait(barrier, nsat - 1 + ntm - 1)

    def each(n, f):
        def body(k, carry):
            f(k)
            return carry
        lax.fori_loop(1, n, body, 0)

    each(nsat, lambda k: weight_copy(k).start())
    for c in range(CHUNKS):
        each(nsat, lambda k: panel_copy(c, k).start())

    root_ref[...] = jnp.zeros_like(root_ref)
    live_all = live_ref[...].astype(jnp.float32)
    pair_lane = lax.broadcasted_iota(jnp.int32, live_all.shape, 1)
    offsets = [ntm // 2] + [k for k in range(ntm - 1, 0, -1) if k != ntm // 2] + [0]
    slots = [(k, r) for k in offsets for r in range(per_owner)]
    owners = {k: lax.rem(t + k, ntm) for k in offsets}

    own_weight.wait()
    each(nsat, lambda k: weight_arrival(k).wait_recv())
    firsts, seconds = [], []
    for n, (k, r) in enumerate(slots):
        pair = owners[k] * per_owner + r
        first, second = members[pair, 0] // nsat, members[pair, 1] // nsat
        firsts.append(first)
        seconds.append(second)
        u = heldw[first].astype(jnp.float32)
        v = heldw[second].astype(jnp.float32)
        live = jnp.sum(jnp.where(pair_lane == pair, live_all, 0.0), axis=1, keepdims=True)
        root_ref[n * epochs:(n + 1) * epochs, :rows] = jnp.sqrt(live * u * v / (u + v))
    root = jnp.transpose(root_ref[...])

    def gram_copy(k):
        return pltpu.make_async_remote_copy(
            src_ref=gram.at[k], dst_ref=arrived.at[k],
            send_sem=gsend.at[k], recv_sem=grecv.at[k],
            device_id={"tm": lax.rem(t + k, ntm)}, device_id_type=MESH)

    for c in range(CHUNKS):
        own_panels[c].wait()
        each(nsat, lambda k: panel_arrival(c, k).wait_recv())
        for n, (k, r) in enumerate(slots):
            for e in range(step):
                at = c * step + e
                column = root[:rows, n * epochs + at:n * epochs + at + 1]
                here = slice(e * rows, (e + 1) * rows)
                scaled[n % 2, here, :params] = (column * held[c][firsts[n], e].astype(jnp.float32)).astype(jnp.bfloat16)
                scaled[n % 2, here, params:] = (column * held[c][seconds[n], e].astype(jnp.float32)).astype(jnp.bfloat16)
            both = scaled[n % 2]
            product = lax.dot_general(both, both, (((0,), (0,)), ((), ())), preferred_element_type=jnp.float32)
            if c > 0:
                product = product + acc[n]
            if c < CHUNKS - 1:
                acc[n] = product
                continue
            base = r * 3 * params
            gram[k, base:base + params] = product[:params, :params]
            gram[k, base + params:base + 2 * params] = -product[:params, params:]
            gram[k, base + 2 * params:base + 3 * params] = product[params:, params:]
            if k > 0 and r == per_owner - 1:
                gram_copy(k).start()

    total = gram[0]
    for k in offsets[:-1]:
        gram_copy(k).wait_recv()
        total = total + arrived[k]
    out_ref[...] = total

    each(nsat, lambda k: weight_copy(k).wait_send())
    for c in range(CHUNKS):
        each(nsat, lambda k: panel_copy(c, k).wait_send())
    for k in offsets[:-1]:
        gram_copy(k).wait_send()


def per_device(panels, weights, pair_members, pair_live):
    nsat, ntm = lax.axis_size("sat"), lax.axis_size("tm")
    sats, epochs, rows, params = panels.shape
    pairs = pair_members.shape[0]
    out_rows = pairs // ntm * 3 * params
    root_rows = -(-pairs * epochs // 128) * 128
    dma = pltpu.SemaphoreType.DMA
    vmem = pl.BlockSpec(memory_space=pltpu.VMEM)
    hbm = pl.BlockSpec(memory_space=pl.ANY)
    return pl.pallas_call(
        functools.partial(kernel, nsat, ntm),
        out_shape=jax.ShapeDtypeStruct((out_rows, params), jnp.float32),
        in_specs=[hbm, hbm, pl.BlockSpec(memory_space=pltpu.SMEM), vmem],
        out_specs=vmem,
        scratch_shapes=[
            *[pltpu.VMEM((nsat, epochs // CHUNKS, rows, params), jnp.bfloat16)] * CHUNKS,
            pltpu.VMEM((nsat, epochs, rows), jnp.bfloat16),
            pltpu.VMEM((root_rows, 128), jnp.float32),
            pltpu.VMEM((2, epochs // CHUNKS * rows, 2 * params), jnp.bfloat16),
            pltpu.VMEM((pairs, 2 * params, 2 * params), jnp.float32),
            pltpu.VMEM((ntm, out_rows, params), jnp.float32),
            pltpu.VMEM((ntm, out_rows, params), jnp.float32),
            dma((CHUNKS, nsat)), dma((CHUNKS, nsat)),
            dma((nsat,)), dma((nsat,)),
            dma((ntm,)), dma((ntm,)),
        ],
        compiler_params=pltpu.CompilerParams(
            collective_id=0, has_side_effects=True, vmem_limit_bytes=48 << 20),
    )(panels, weights, pair_members, pair_live)


def solution(mesh):
    in_specs = (P("sat", "tm", None, None), P("sat", "tm", None), P("sat", None), P("tm", "sat"))
    out_specs = P(("sat", "tm"), None)
    return jax.shard_map(
        per_device, mesh=mesh, in_specs=in_specs, out_specs=out_specs, check_vma=False
    )
```

```python
import functools
import jax
import jax.numpy as jnp
from jax import lax
from jax.experimental import pallas as pl
from jax.experimental.pallas import tpu as pltpu
from jax.sharding import PartitionSpec as P

MESH = pl.DeviceIdType.MESH
CHUNKS = 4


def kernel(nsat, ntm, panels, weights, members, live_ref, out_ref, *scratch):
    held = scratch[:CHUNKS]
    (heldw, root_ref, scaled, acc, gram, arrived,
     psend, precv, wsend, wrecv, gsend, grecv) = scratch[CHUNKS:]
    epochs, rows, params = panels.shape[1:]
    pairs = members.shape[1]
    per_owner = pairs // ntm
    step = epochs // CHUNKS
    s = lax.axis_index("sat")
    t = lax.axis_index("tm")

    barrier = pltpu.get_barrier_semaphore()

    def greet(axis, me, n):
        def body(k, carry):
            pl.semaphore_signal(barrier, inc=1, device_id={axis: lax.rem(me + k, n)}, device_id_type=MESH)
            return carry
        lax.fori_loop(1, n, body, 0)

    greet("sat", s, nsat)
    greet("tm", t, ntm)

    def weight_copy(k):
        dest = lax.rem(s + k, nsat)
        return pltpu.make_async_remote_copy(
            src_ref=weights.at[dest], dst_ref=heldw.at[s],
            send_sem=wsend.at[k], recv_sem=wrecv.at[k],
            device_id={"sat": dest}, device_id_type=MESH)

    def weight_arrival(k):
        source = lax.rem(s + nsat - k, nsat)
        return pltpu.make_async_remote_copy(
            src_ref=weights.at[s], dst_ref=heldw.at[source],
            send_sem=wsend.at[k], recv_sem=wrecv.at[k],
            device_id={"sat": source}, device_id_type=MESH)

    def panel_copy(c, k):
        dest = lax.rem(s + k, nsat)
        part = pl.ds(c * step, step)
        return pltpu.make_async_remote_copy(
            src_ref=panels.at[dest, part], dst_ref=held[c].at[s],
            send_sem=psend.at[c, k], recv_sem=precv.at[c, k],
            device_id={"sat": dest}, device_id_type=MESH)

    def panel_arrival(c, k):
        source = lax.rem(s + nsat - k, nsat)
        part = pl.ds(c * step, step)
        return pltpu.make_async_remote_copy(
            src_ref=panels.at[s, part], dst_ref=held[c].at[source],
            send_sem=psend.at[c, k], recv_sem=precv.at[c, k],
            device_id={"sat": source}, device_id_type=MESH)

    own_panels = [
        pltpu.make_async_copy(panels.at[s, pl.ds(c * step, step)], held[c].at[s], psend.at[c, 0])
        for c in range(CHUNKS)
    ]
    own_weight = pltpu.make_async_copy(weights.at[s], heldw.at[s], wsend.at[0])
    for copy in own_panels:
        copy.start()
    own_weight.start()

    pl.semaphore_wait(barrier, nsat - 1 + ntm - 1)

    def each(n, f):
        def body(k, carry):
            f(k)
            return carry
        lax.fori_loop(1, n, body, 0)

    each(nsat, lambda k: weight_copy(k).start())
    for c in range(CHUNKS):
        each(nsat, lambda k: panel_copy(c, k).start())

    root_ref[...] = jnp.zeros_like(root_ref)
    root_ref[:pairs, :epochs] = live_ref[...].astype(jnp.float32)
    live_all = jnp.transpose(root_ref[:128])[:epochs]
    pair_lane = lax.broadcasted_iota(jnp.int32, live_all.shape, 1)
    offsets = [ntm // 2] + [k for k in range(ntm - 1, 0, -1) if k != ntm // 2] + [0]
    slots = [(k, r) for k in offsets for r in range(per_owner)]
    owners = {k: lax.rem(t + k, ntm) for k in offsets}

    row = lax.broadcasted_iota(jnp.int32, (params, params), 0)
    col = lax.broadcasted_iota(jnp.int32, (params, params), 1)
    lower, on_diagonal = row >= col, row == col

    own_weight.wait()
    each(nsat, lambda k: weight_arrival(k).wait_recv())
    firsts, seconds = [], []
    for n, (k, r) in enumerate(slots):
        pair = owners[k] * per_owner + r
        first, second = members[0, pair] // nsat, members[1, pair] // nsat
        firsts.append(first)
        seconds.append(second)
        u = heldw[first].astype(jnp.float32)
        v = heldw[second].astype(jnp.float32)
        live = jnp.sum(jnp.where(pair_lane == pair, live_all, 0.0), axis=1, keepdims=True)
        root_ref[n * epochs:(n + 1) * epochs, :rows] = jnp.sqrt(live * u * v / (u + v))
    root = jnp.transpose(root_ref[...])

    def gram_copy(k):
        return pltpu.make_async_remote_copy(
            src_ref=gram.at[k], dst_ref=arrived.at[k],
            send_sem=gsend.at[k], recv_sem=grecv.at[k],
            device_id={"tm": lax.rem(t + k, ntm)}, device_id_type=MESH)

    for c in range(CHUNKS):
        own_panels[c].wait()
        each(nsat, lambda k: panel_arrival(c, k).wait_recv())
        for n, (k, r) in enumerate(slots):
            for e in range(step):
                at = c * step + e
                column = root[:rows, n * epochs + at:n * epochs + at + 1]
                here = slice(e * rows, (e + 1) * rows)
                scaled[n % 2, here, :params] = (column * held[c][firsts[n], e].astype(jnp.float32)).astype(jnp.bfloat16)
                scaled[n % 2, here, params:] = (column * held[c][seconds[n], e].astype(jnp.float32)).astype(jnp.bfloat16)
            both = scaled[n % 2]
            product = lax.dot_general(both, both, (((0,), (0,)), ((), ())), preferred_element_type=jnp.float32)
            if c > 0:
                product = product + acc[n]
            if c < CHUNKS - 1:
                acc[n] = product
                continue
            second_gram = product[params:, params:]
            gram[k, r, :params] = jnp.where(lower, product[:params, :params], second_gram)
            gram[k, r, params:2 * params] = -product[:params, params:]
            diagonal = jnp.sum(jnp.where(on_diagonal, second_gram, 0.0), axis=0, keepdims=True)
            gram[k, r, 2 * params:] = jnp.broadcast_to(diagonal, (8, params))
            if k > 0 and r == per_owner - 1:
                gram_copy(k).start()

    total = gram[0]
    for k in offsets[:-1]:
        gram_copy(k).wait_recv()
        total = total + arrived[k]
    for r in range(per_owner):
        base = r * 3 * params
        packed = total[r, :params]
        mirrored = jnp.transpose(packed)
        out_ref[base:base + params] = jnp.where(lower, packed, mirrored)
        out_ref[base + params:base + 2 * params] = total[r, params:2 * params]
        second_gram = jnp.where(on_diagonal, total[r, 2 * params:2 * params + 1], mirrored)
        out_ref[base + 2 * params:base + 3 * params] = jnp.where(row < col, packed, second_gram)

    each(nsat, lambda k: weight_copy(k).wait_send())
    for c in range(CHUNKS):
        each(nsat, lambda k: panel_copy(c, k).wait_send())
    for k in offsets[:-1]:
        gram_copy(k).wait_send()


def per_device(panels, weights, pair_members, pair_live):
    nsat, ntm = lax.axis_size("sat"), lax.axis_size("tm")
    sats, epochs, rows, params = panels.shape
    pairs = pair_members.shape[0]
    out_rows = pairs // ntm * 3 * params
    root_rows = -(-pairs * epochs // 128) * 128
    dma = pltpu.SemaphoreType.DMA
    vmem = pl.BlockSpec(memory_space=pltpu.VMEM)
    hbm = pl.BlockSpec(memory_space=pltpu.HBM)
    return pl.pallas_call(
        functools.partial(kernel, nsat, ntm),
        out_shape=jax.ShapeDtypeStruct((out_rows, params), jnp.float32),
        in_specs=[hbm, hbm, pl.BlockSpec(memory_space=pltpu.SMEM), vmem],
        out_specs=vmem,
        scratch_shapes=[
            *[pltpu.VMEM((nsat, epochs // CHUNKS, rows, params), jnp.bfloat16)] * CHUNKS,
            pltpu.VMEM((nsat, epochs, rows), jnp.bfloat16),
            pltpu.VMEM((root_rows, 128), jnp.float32),
            pltpu.VMEM((2, epochs // CHUNKS * rows, 2 * params), jnp.bfloat16),
            pltpu.VMEM((pairs, 2 * params, 2 * params), jnp.float32),
            pltpu.VMEM((ntm, pairs // ntm, 2 * params + 8, params), jnp.float32),
            pltpu.VMEM((ntm, pairs // ntm, 2 * params + 8, params), jnp.float32),
            dma((CHUNKS, nsat)), dma((CHUNKS, nsat)),
            dma((nsat,)), dma((nsat,)),
            dma((ntm,)), dma((ntm,)),
        ],
        compiler_params=pltpu.CompilerParams(
            collective_id=0, has_side_effects=True, vmem_limit_bytes=60 << 20),
    )(panels, weights, pair_members.T, pair_live.T)


def solution(mesh):
    in_specs = (P("sat", "tm", None, None), P("sat", "tm", None), P("sat", None), P("tm", "sat"))
    out_specs = P(("sat", "tm"), None)
    return jax.shard_map(
        per_device, mesh=mesh, in_specs=in_specs, out_specs=out_specs, check_vma=False
    )
```

```python
import functools
import jax
import jax.numpy as jnp
from jax import lax
from jax.experimental import pallas as pl
from jax.experimental.pallas import tpu as pltpu
from jax.sharding import PartitionSpec as P

MESH = pl.DeviceIdType.MESH


def chunk_sizes(epochs):
    count = min(epochs, 4)
    return [epochs * (c + 1) // count - epochs * c // count for c in range(count)]


def kernel(nsat, ntm, panels, weights, members, live_ref, out_ref, *scratch):
    epochs, rows, params = panels.shape[1:]
    sizes = chunk_sizes(epochs)
    chunks = range(len(sizes))
    starts = [sum(sizes[:c]) for c in chunks]
    held, scaled, arrived = (scratch[n * len(sizes):(n + 1) * len(sizes)] for n in range(3))
    heldw, root_ref, psend, precv, wsend, wrecv, fsend, frecv = scratch[3 * len(sizes):]
    pairs = members.shape[1]
    per_owner = pairs // ntm
    s = lax.axis_index("sat")
    t = lax.axis_index("tm")

    barrier = pltpu.get_barrier_semaphore()

    def greet(axis, me, n):
        def body(k, carry):
            pl.semaphore_signal(barrier, inc=1, device_id={axis: lax.rem(me + k, n)}, device_id_type=MESH)
            return carry
        lax.fori_loop(1, n, body, 0)

    greet("sat", s, nsat)
    greet("tm", t, ntm)

    def weight_copy(k):
        dest = lax.rem(s + k, nsat)
        return pltpu.make_async_remote_copy(
            src_ref=weights.at[dest], dst_ref=heldw.at[s],
            send_sem=wsend.at[k], recv_sem=wrecv.at[k],
            device_id={"sat": dest}, device_id_type=MESH)

    def weight_arrival(k):
        source = lax.rem(s + nsat - k, nsat)
        return pltpu.make_async_remote_copy(
            src_ref=weights.at[s], dst_ref=heldw.at[source],
            send_sem=wsend.at[k], recv_sem=wrecv.at[k],
            device_id={"sat": source}, device_id_type=MESH)

    def panel_copy(c, k):
        dest = lax.rem(s + k, nsat)
        part = pl.ds(starts[c], sizes[c])
        return pltpu.make_async_remote_copy(
            src_ref=panels.at[dest, part], dst_ref=held[c].at[s],
            send_sem=psend.at[c, k], recv_sem=precv.at[c, k],
            device_id={"sat": dest}, device_id_type=MESH)

    def panel_arrival(c, k):
        source = lax.rem(s + nsat - k, nsat)
        part = pl.ds(starts[c], sizes[c])
        return pltpu.make_async_remote_copy(
            src_ref=panels.at[s, part], dst_ref=held[c].at[source],
            send_sem=psend.at[c, k], recv_sem=precv.at[c, k],
            device_id={"sat": source}, device_id_type=MESH)

    own_panels = [
        pltpu.make_async_copy(panels.at[s, pl.ds(starts[c], sizes[c])], held[c].at[s], psend.at[c, 0])
        for c in chunks
    ]
    own_weight = pltpu.make_async_copy(weights.at[s], heldw.at[s], wsend.at[0])
    for copy in own_panels:
        copy.start()
    own_weight.start()

    pl.semaphore_wait(barrier, nsat - 1 + ntm - 1)

    def each(n, f):
        def body(k, carry):
            f(k)
            return carry
        lax.fori_loop(1, n, body, 0)

    each(nsat, lambda k: weight_copy(k).start())
    for c in chunks:
        each(nsat, lambda k: panel_copy(c, k).start())

    root_ref[...] = jnp.zeros_like(root_ref)
    root_ref[:pairs, :epochs] = live_ref[...].astype(jnp.float32)
    live_all = jnp.transpose(root_ref[:128])[:epochs]
    pair_lane = lax.broadcasted_iota(jnp.int32, live_all.shape, 1)
    offsets = [ntm // 2] + [k for k in range(ntm - 1, 0, -1) if k != ntm // 2] + [0]
    slots = [(k, r) for k in offsets for r in range(per_owner)]
    owners = {k: lax.rem(t + k, ntm) for k in offsets}

    own_weight.wait()
    each(nsat, lambda k: weight_arrival(k).wait_recv())
    firsts, seconds = [], []
    for n, (k, r) in enumerate(slots):
        pair = owners[k] * per_owner + r
        first, second = members[0, pair] // nsat, members[1, pair] // nsat
        firsts.append(first)
        seconds.append(second)
        u = heldw[first].astype(jnp.float32)
        v = heldw[second].astype(jnp.float32)
        live = jnp.sum(jnp.where(pair_lane == pair, live_all, 0.0), axis=1, keepdims=True)
        root_ref[n * epochs:(n + 1) * epochs, :rows] = jnp.sqrt(live * u * v / (u + v))
    root = jnp.transpose(root_ref[...])

    def forward(c, k):
        return pltpu.make_async_remote_copy(
            src_ref=scaled[c].at[k], dst_ref=arrived[c].at[k],
            send_sem=fsend.at[c, k], recv_sem=frecv.at[c, k],
            device_id={"tm": lax.rem(t + k, ntm)}, device_id_type=MESH)

    totals = [jnp.zeros((2 * params, 2 * params), jnp.float32)] * per_owner

    def add_rows(block):
        for r in range(per_owner):
            both = block[r]
            totals[r] += lax.dot_general(both, both, (((0,), (0,)), ((), ())), preferred_element_type=jnp.float32)

    def add_arrived(c):
        for k in reversed(offsets[:-1]):
            forward(c, k).wait_recv()
            add_rows(arrived[c].at[k])

    for c in chunks:
        own_panels[c].wait()
        each(nsat, lambda k: panel_arrival(c, k).wait_recv())
        for n, (k, r) in enumerate(slots):
            for e in range(sizes[c]):
                at = n * epochs + starts[c] + e
                column = root[:rows, at:at + 1]
                here = slice(e * rows, (e + 1) * rows)
                scaled[c][k, r, here, :params] = (column * held[c][firsts[n], e].astype(jnp.float32)).astype(jnp.bfloat16)
                scaled[c][k, r, here, params:] = (column * held[c][seconds[n], e].astype(jnp.float32)).astype(jnp.bfloat16)
            if k > 0 and r == per_owner - 1:
                forward(c, k).start()
        add_rows(scaled[c].at[0])
    for c in chunks:
        add_arrived(c)

    for r in range(per_owner):
        base = r * 3 * params
        out_ref[base:base + params] = totals[r][:params, :params]
        out_ref[base + params:base + 2 * params] = -totals[r][:params, params:]
        out_ref[base + 2 * params:base + 3 * params] = totals[r][params:, params:]

    each(nsat, lambda k: weight_copy(k).wait_send())
    for c in chunks:
        each(nsat, lambda k: panel_copy(c, k).wait_send())
        for k in offsets[:-1]:
            forward(c, k).wait_send()


def per_device(panels, weights, pair_members, pair_live):
    nsat, ntm = lax.axis_size("sat"), lax.axis_size("tm")
    sats, epochs, rows, params = panels.shape
    pairs = pair_members.shape[0]
    sizes = chunk_sizes(epochs)
    out_rows = pairs // ntm * 3 * params
    root_rows = -(-pairs * epochs // 128) * 128
    dma = pltpu.SemaphoreType.DMA
    vmem = pl.BlockSpec(memory_space=pltpu.VMEM)
    hbm = pl.BlockSpec(memory_space=pltpu.HBM)
    return pl.pallas_call(
        functools.partial(kernel, nsat, ntm),
        out_shape=jax.ShapeDtypeStruct((out_rows, params), jnp.float32),
        in_specs=[hbm, hbm, pl.BlockSpec(memory_space=pltpu.SMEM), vmem],
        out_specs=vmem,
        scratch_shapes=[
            *[pltpu.VMEM((nsat, size, rows, params), jnp.bfloat16) for size in sizes],
            *[pltpu.VMEM((ntm, pairs // ntm, size * rows, 2 * params), jnp.bfloat16) for size in sizes] * 2,
            pltpu.VMEM((nsat, epochs, rows), jnp.bfloat16),
            pltpu.VMEM((root_rows, 128), jnp.float32),
            dma((len(sizes), nsat)), dma((len(sizes), nsat)),
            dma((nsat,)), dma((nsat,)),
            dma((len(sizes), ntm)), dma((len(sizes), ntm)),
        ],
        compiler_params=pltpu.CompilerParams(
            collective_id=0, has_side_effects=True, vmem_limit_bytes=60 << 20),
    )(panels, weights, pair_members.T, pair_live.T)


def solution(mesh):
    in_specs = (P("sat", "tm", None, None), P("sat", "tm", None), P("sat", None), P("tm", "sat"))
    out_specs = P(("sat", "tm"), None)
    return jax.shard_map(
        per_device, mesh=mesh, in_specs=in_specs, out_specs=out_specs, check_vma=False
    )
```

```python
import functools
import jax
import jax.numpy as jnp
from jax import lax
from jax.experimental import pallas as pl
from jax.experimental.pallas import tpu as pltpu
from jax.sharding import PartitionSpec as P

MESH = pl.DeviceIdType.MESH


def chunk_sizes(epochs):
    count = min(epochs, 4)
    return [epochs * (c + 1) // count - epochs * c // count for c in range(count)]


def partner(me, k, n):
    place, other = 1, 0
    while place < n:
        other = other + lax.rem(me // place + k // place, 2) * place
        place *= 2
    return other


def kernel(nsat, ntm, panels, weights, members, live_ref, out_ref, *scratch):
    epochs, rows, params = panels.shape[1:]
    sizes = chunk_sizes(epochs)
    chunks = range(len(sizes))
    starts = [sum(sizes[:c]) for c in chunks]
    held, scaled, arrived = (scratch[n * len(sizes):(n + 1) * len(sizes)] for n in range(3))
    heldw, root_ref, psend, precv, wsend, wrecv, fsend, frecv = scratch[3 * len(sizes):]
    pairs = members.shape[1]
    per_owner = pairs // ntm
    s = lax.axis_index("sat")
    t = lax.axis_index("tm")

    barrier = pltpu.get_barrier_semaphore()

    def greet(axis, me, n):
        def body(k, carry):
            pl.semaphore_signal(barrier, inc=1, device_id={axis: lax.rem(me + k, n)}, device_id_type=MESH)
            return carry
        lax.fori_loop(1, n, body, 0, unroll=True)

    greet("sat", s, nsat)
    greet("tm", t, ntm)

    def weight_copy(k):
        dest = lax.rem(s + k, nsat)
        return pltpu.make_async_remote_copy(
            src_ref=weights.at[dest], dst_ref=heldw.at[s],
            send_sem=wsend.at[k], recv_sem=wrecv.at[k],
            device_id={"sat": dest}, device_id_type=MESH)

    def weight_arrival(k):
        source = lax.rem(s + nsat - k, nsat)
        return pltpu.make_async_remote_copy(
            src_ref=weights.at[s], dst_ref=heldw.at[source],
            send_sem=wsend.at[k], recv_sem=wrecv.at[k],
            device_id={"sat": source}, device_id_type=MESH)

    def panel_copy(c, k):
        dest = lax.rem(s + k, nsat)
        part = pl.ds(starts[c], sizes[c])
        return pltpu.make_async_remote_copy(
            src_ref=panels.at[dest, part], dst_ref=held[c].at[s],
            send_sem=psend.at[c, k], recv_sem=precv.at[c, k],
            device_id={"sat": dest}, device_id_type=MESH)

    def panel_arrival(c, k):
        source = lax.rem(s + nsat - k, nsat)
        part = pl.ds(starts[c], sizes[c])
        return pltpu.make_async_remote_copy(
            src_ref=panels.at[s, part], dst_ref=held[c].at[source],
            send_sem=psend.at[c, k], recv_sem=precv.at[c, k],
            device_id={"sat": source}, device_id_type=MESH)

    own_panels = [
        pltpu.make_async_copy(panels.at[s, pl.ds(starts[c], sizes[c])], held[c].at[s], psend.at[c, 0])
        for c in chunks
    ]
    own_weight = pltpu.make_async_copy(weights.at[s], heldw.at[s], wsend.at[0])
    for copy in own_panels:
        copy.start()
    own_weight.start()

    pl.semaphore_wait(barrier, nsat - 1 + ntm - 1)

    def each(n, f):
        def body(k, carry):
            f(k)
            return carry
        lax.fori_loop(1, n, body, 0, unroll=True)

    for c in chunks:
        each(nsat, lambda k: panel_copy(c, k).start())
        if c == 0:
            each(nsat, lambda k: weight_copy(k).start())

    root_ref[...] = jnp.zeros_like(root_ref)
    root_ref[:pairs, :epochs] = live_ref[...].astype(jnp.float32)
    live_all = jnp.transpose(root_ref[:128])[:epochs]
    pair_lane = lax.broadcasted_iota(jnp.int32, live_all.shape, 1)
    offsets = list(range(2, ntm)) + [1, 0]
    slots = [(k, r) for k in offsets for r in range(per_owner)]
    owners = {k: partner(t, k, ntm) for k in offsets}

    own_weight.wait()
    each(nsat, lambda k: weight_arrival(k).wait_recv())
    firsts, seconds = [], []
    for n, (k, r) in enumerate(slots):
        pair = owners[k] * per_owner + r
        first, second = members[0, pair] // nsat, members[1, pair] // nsat
        firsts.append(first)
        seconds.append(second)
        u = heldw[first].astype(jnp.float32)
        v = heldw[second].astype(jnp.float32)
        live = jnp.sum(jnp.where(pair_lane == pair, live_all, 0.0), axis=1, keepdims=True)
        root_ref[n * epochs:(n + 1) * epochs, :rows] = jnp.sqrt(live * u * v / (u + v))
    root = jnp.transpose(root_ref[...])

    def forward(c, k):
        return pltpu.make_async_remote_copy(
            src_ref=scaled[c].at[k], dst_ref=arrived[c].at[k],
            send_sem=fsend.at[c, k], recv_sem=frecv.at[c, k],
            device_id={"tm": owners[k]}, device_id_type=MESH)

    totals = [jnp.zeros((2 * params, 2 * params), jnp.float32)] * per_owner

    def add_rows(block):
        for r in range(per_owner):
            both = block[r]
            totals[r] += lax.dot_general(both, both, (((0,), (0,)), ((), ())), preferred_element_type=jnp.float32)

    def add_arrived(c):
        for k in reversed(offsets[:-1]):
            forward(c, k).wait_recv()
            add_rows(arrived[c].at[k])

    for c in chunks:
        own_panels[c].wait()
        each(nsat, lambda k: panel_arrival(c, k).wait_recv())
        for n, (k, r) in enumerate(slots):
            for e in range(sizes[c]):
                at = n * epochs + starts[c] + e
                column = root[:rows, at:at + 1]
                here = slice(e * rows, (e + 1) * rows)
                scaled[c][k, r, here, :params] = (column * held[c][firsts[n], e].astype(jnp.float32)).astype(jnp.bfloat16)
                scaled[c][k, r, here, params:] = (column * held[c][seconds[n], e].astype(jnp.float32)).astype(jnp.bfloat16)
            if k > 0 and r == per_owner - 1:
                forward(c, k).start()
        add_rows(scaled[c].at[0])
    for c in chunks:
        add_arrived(c)

    for r in range(per_owner):
        base = r * 3 * params
        out_ref[base:base + params] = totals[r][:params, :params]
        out_ref[base + params:base + 2 * params] = -totals[r][:params, params:]
        out_ref[base + 2 * params:base + 3 * params] = totals[r][params:, params:]

    each(nsat, lambda k: weight_copy(k).wait_send())
    for c in chunks:
        each(nsat, lambda k: panel_copy(c, k).wait_send())
        for k in offsets[:-1]:
            forward(c, k).wait_send()


def per_device(panels, weights, pair_members, pair_live):
    nsat, ntm = lax.axis_size("sat"), lax.axis_size("tm")
    sats, epochs, rows, params = panels.shape
    pairs = pair_members.shape[0]
    sizes = chunk_sizes(epochs)
    out_rows = pairs // ntm * 3 * params
    root_rows = -(-pairs * epochs // 128) * 128
    dma = pltpu.SemaphoreType.DMA
    vmem = pl.BlockSpec(memory_space=pltpu.VMEM)
    hbm = pl.BlockSpec(memory_space=pltpu.HBM)
    return pl.pallas_call(
        functools.partial(kernel, nsat, ntm),
        out_shape=jax.ShapeDtypeStruct((out_rows, params), jnp.float32),
        in_specs=[hbm, hbm, pl.BlockSpec(memory_space=pltpu.SMEM), vmem],
        out_specs=vmem,
        scratch_shapes=[
            *[pltpu.VMEM((nsat, size, rows, params), jnp.bfloat16) for size in sizes],
            *[pltpu.VMEM((ntm, pairs // ntm, size * rows, 2 * params), jnp.bfloat16) for size in sizes] * 2,
            pltpu.VMEM((nsat, epochs, rows), jnp.bfloat16),
            pltpu.VMEM((root_rows, 128), jnp.float32),
            dma((len(sizes), nsat)), dma((len(sizes), nsat)),
            dma((nsat,)), dma((nsat,)),
            dma((len(sizes), ntm)), dma((len(sizes), ntm)),
        ],
        compiler_params=pltpu.CompilerParams(
            collective_id=0, has_side_effects=True, vmem_limit_bytes=60 << 20),
    )(panels, weights, pair_members.T, pair_live.T)


def solution(mesh):
    in_specs = (P("sat", "tm", None, None), P("sat", "tm", None), P("sat", None), P("tm", "sat"))
    out_specs = P(("sat", "tm"), None)
    return jax.shard_map(
        per_device, mesh=mesh, in_specs=in_specs, out_specs=out_specs, check_vma=False
    )
```
